32 devices in a mesh: segment: 2 (over core), expert: 8 (over z, y), dp: 2 (over x).
Axes of the slice: x: 2, y: 2, z: 4, core: 2. Of those that a mesh axis runs over, the one named last changes fastest.
Arguments:
- moe_input: bfloat16 [2, 1024, 2688], P('segment', 'expert', 'dp'), may hold values from -64 to 64
- norm_gain: float32 [2688], replicated, may hold values from 0.1 to 1.9
- routes: int32 [2, 1024, 6], P('segment', 'expert'), may hold values from 0 to 15, all different within a row; in each aligned block of 128 rows (0 to 127, 128 to 255, ..., all dimensions but the last counted through in order) at most 54 rows name the same one
- route_scores: float32 [2, 1024, 6], P('segment', 'expert'), may hold values from -8 to 8
- w_up: bfloat16 [16, 2688, 1856], P('expert', None, 'dp'), may hold values from -0.125 to 0.125
- w_down: bfloat16 [16, 1856, 2688], P('expert', None, 'dp'), may hold values from -0.125 to 0.125
- queries: bfloat16 [2, 1024, 2048], P('segment', 'expert', 'dp'), may hold values from -100 to 100
- keys: bfloat16 [2, 1024, 256], P('segment', 'expert'), may hold values from -6 to 6
- values: bfloat16 [2, 1024, 256], P('segment', 'expert'), may hold values from -6 to 6
- out_grad: bfloat16 [2, 1024, 2688], P('segment', 'expert'), may hold values from -6 to 6
- w_query: bfloat16 [2688, 2048], P(None, 'dp'), may hold values from -0.125 to 0.125
- w_key: bfloat16 [2688, 256], replicated, may hold values from -0.125 to 0.125
- w_value: bfloat16 [2688, 256], replicated, may hold values from -0.125 to 0.125
- w_out: bfloat16 [2048, 2688], P('dp'), may hold values from -0.125 to 0.125
Outputs:
- moe_next: bfloat16 [2, 1024, 2688], P('segment', 'expert', 'dp')
- grad_prev: bfloat16 [2, 1024, 2688], P('segment', 'expert', 'dp')
The draws below stay inside these ranges and needn't reach their ends.
Inputs may be any that keep to these rules, and one draw needn't show every extreme that they name: `routes`: each row names 6 different experts. Among the 128 rows of one sequence no expert is named more than 54 times, a bound that some block reaches; every expert is named by some row.
All inputs are finite; a program needn't handle non-finite values.
Results may differ from the reference program's by a relative error of at most 0.028.
Values may be sent and summed in bfloat16 or wider, within the bound.
No kernel may reach another device: no remote copies, remote signals or barrier semaphores. Data moves between devices by JAX's collectives and lax.ppermute only.
A program may use at most 128 MiB of HBM per device.

```python
import math
import jax
import jax.numpy as jnp
import numpy as np
from jax import lax

D = 2688
HID = 1856
HEADS = 16
KV_HEADS = 2
HEAD_DIM = 128
TOPK = 6
TOK_DEV = 128
SEGMENTS = 2
TOKENS = 1024
EXPERTS = 16
CAP = 54
HEAD_BLOCK = 8
QW = 2048
KVW = 256
N_EXPERT = 8
N_DP = 2


def draw_moe_input(key, part):
    full_shape = (SEGMENTS, TOKENS, D)
    base_key = jax.random.fold_in(key, 21)
    column_key = jax.random.fold_in(key, 22)
    row_key = jax.random.fold_in(key, 23)
    raw_values = jax.random.truncated_normal(base_key, -4.0, 4.0, full_shape, jnp.float32)
    column_scale = jnp.exp(jax.random.uniform(column_key, (SEGMENTS, 1, D), jnp.float32, math.log(0.3), math.log(3.0)))
    row_scale = jnp.exp(jax.random.uniform(row_key, (SEGMENTS, TOKENS, 1), jnp.float32, math.log(0.5), math.log(5.0)))
    return (raw_values * column_scale * row_scale).astype(jnp.bfloat16)


def attention_pair(key):
    sequences = TOKENS // TOK_DEV
    query_key = jax.random.fold_in(key, 31)
    keys_key = jax.random.fold_in(key, 32)
    keys_all = jax.random.truncated_normal(keys_key, -5.0, 5.0, (SEGMENTS, sequences, TOK_DEV, KV_HEADS, HEAD_DIM), jnp.float32)
    queries_all = jax.random.truncated_normal(query_key, -5.0, 5.0, (SEGMENTS, sequences, TOK_DEV, HEADS, HEAD_DIM), jnp.float32)
    return (queries_all.reshape(SEGMENTS, TOKENS, HEADS * HEAD_DIM), keys_all.reshape(SEGMENTS, TOKENS, KV_HEADS * HEAD_DIM))


def draw_queries(key, part):
    return attention_pair(key)[0].astype(jnp.bfloat16)


def draw_keys(key, part):
    return attention_pair(key)[1].astype(jnp.bfloat16)


def level_of(rng, extent, shards, low, top_value):
    def one(dim, blocks):
        heights = jax.random.uniform(jax.random.fold_in(jax.random.fold_in(rng, 6), dim), (blocks,), jnp.float32, low / len(shards), top_value / len(shards))
        return jnp.repeat(jnp.exp(heights), extent[dim] // blocks).reshape((-1,) + (1,) * (len(extent) - dim - 1))

    level = one(*shards[0])
    for cut in shards[1:]:
        level = level * one(*cut)
    return level


def routed_block(rng, own, number, rows, number_of, top, bound, lean):
    order = jax.random.permutation(rng, number_of)
    packed, usual = shares(number_of, rows * top, bound, lean, True), shares(number_of, rows * top, bound, lean, False)
    places = jnp.arange(number_of)

    def named(lengths, offset_by):
        used = int((lengths > 0).sum())
        fixed = max(1, used // 4)
        shifted = fixed + (places - fixed + offset_by * (used - fixed)) % max(1, number_of - fixed)
        return jnp.zeros((number_of,), jnp.int32).at[order[jnp.where(places < fixed, places, shifted)]].set(jnp.asarray(lengths, jnp.int32))

    lengths = jnp.where(number % 4 == 0, named(packed, number // 4), named(usual, number - number // 4 - 1))
    mixed = jax.random.permutation(jax.random.fold_in(own, 3), number_of)
    donor, taker = mixed[0:number_of // 2 * 2:2], mixed[1:number_of // 2 * 2:2]
    margin = jnp.minimum(lengths[donor] - 1, bound - lengths[taker]) // 2
    margin = jnp.where((donor == order[0]) | (taker == order[0]) | (lengths[taker] == 0), 0, jnp.maximum(margin, 0))
    shifted = jax.random.randint(jax.random.fold_in(own, 4), (number_of // 2,), 0, 1 << 20) % (margin + 1)
    lengths = lengths.at[donor].add(-shifted).at[taker].add(shifted)
    members = jnp.searchsorted(jnp.cumsum(lengths), jnp.arange(rows * top), side="right").astype(jnp.int32)
    grid = members.reshape(top, rows).T
    grid = grid[jax.random.permutation(jax.random.fold_in(own, 1), rows)]
    offset_by = jax.random.randint(jax.random.fold_in(own, 2), (rows, 1), 0, top)
    return jnp.take_along_axis(grid, (jnp.arange(top)[None, :] + offset_by) % top, axis=1)


def shares(count, total, reach, slope, full):
    portions = [(1 << 20) // math.isqrt(standing ** slope) + 1 for standing in range(1, count + 1)]
    largest = reach if full else min(reach, max(-(-total // count), total * portions[0] // sum(portions)))
    least = 1 if total - largest >= count - 1 else 0
    counts, rest = [largest] + [least] * (count - 1), total - largest - least * (count - 1)
    while rest > 0:
        movable = [i for i in range(1, count) if counts[i] < largest] or [i for i in range(1, count) if counts[i] < reach]
        whole, remaining = sum([portions[i] for i in movable]), rest
        for i in movable:
            addition = min(reach - counts[i], max(1, remaining * portions[i] // whole), rest)
            counts[i] = counts[i] + addition
            rest = rest - addition
    return np.array(counts)


def noise(own_key, shape, spread, bound, cuts=(), kind=jnp.bfloat16):
    values = spread * jax.random.normal(own_key, shape, jnp.float32)
    if cuts:
        values = values * level_of(own_key, shape, cuts, -0.22, 0.18)
    return jnp.clip(values, -bound, bound).astype(kind)


def setup_inputs(seed: int = 0) -> dict:
    streams_of = jax.random.split(jax.random.key(seed), 15)
    moe_input = draw_moe_input(jax.random.fold_in(streams_of[14], 71), 0)
    norm_gain = jnp.clip(1.0 + 0.18 * jax.random.normal(streams_of[1], (D,), jnp.float32), 0.1, 1.9)
    routes_keys = jax.random.split(jax.random.fold_in(streams_of[2], 1), SEGMENTS * TOKENS // TOK_DEV)
    routes_turns = jax.random.permutation(jax.random.fold_in(streams_of[2], 3), SEGMENTS * TOKENS // TOK_DEV)
    routes = jax.vmap(lambda own, number: routed_block(jax.random.fold_in(streams_of[2], 2), own, number, TOK_DEV, EXPERTS, TOPK, CAP, 2))(routes_keys, routes_turns).reshape((SEGMENTS, TOKENS, TOPK))
    route_scores = noise(streams_of[3], (SEGMENTS, TOKENS, TOPK), 2.0, 8.0, ((0, 2), (1, 8)), jnp.float32)
    w_up = noise(streams_of[4], (EXPERTS, D, HID), D ** -0.5, 0.125, ((0, 8), (2, 2)))
    w_down = noise(streams_of[5], (EXPERTS, HID, D), HID ** -0.5, 0.125, ((0, 8), (2, 2)))
    queries = draw_queries(jax.random.fold_in(streams_of[14], 71), 0)
    keys = draw_keys(jax.random.fold_in(streams_of[14], 71), 0)
    values = noise(streams_of[8], (SEGMENTS, TOKENS, KVW), 1.0, 6.0, ((0, 2), (1, 8)))
    out_grad = noise(streams_of[9], (SEGMENTS, TOKENS, D), 1.0, 6.0, ((0, 2), (1, 8)))
    w_query = noise(streams_of[10], (D, QW), D ** -0.5, 0.125, ((1, 2),))
    w_key = noise(streams_of[11], (D, KVW), D ** -0.5, 0.125)
    w_value = noise(streams_of[12], (D, KVW), D ** -0.5, 0.125)
    w_out = noise(streams_of[13], (QW, D), QW ** -0.5, 0.125, ((0, 2),))
    return {"moe_input": moe_input, "norm_gain": norm_gain, "routes": routes, "route_scores": route_scores, "w_up": w_up, "w_down": w_down, "queries": queries, "keys": keys, "values": values, "out_grad": out_grad, "w_query": w_query, "w_key": w_key, "w_value": w_value, "w_out": w_out}


NORM_EPSILON = 1e-05

def settle(value):
    return lax.optimization_barrier(value.astype(jnp.bfloat16)).astype(jnp.float32)

def slot_places(block_routes):
    flat_routes = block_routes.reshape(-1)
    expert_hits = (flat_routes[:, None] == jnp.arange(EXPERTS, dtype=jnp.int32)[None, :]).astype(jnp.int32)
    earlier = jnp.cumsum(expert_hits, axis=0) - expert_hits
    return lax.optimization_barrier(jnp.sum(earlier * expert_hits, axis=1)).reshape(block_routes.shape).astype(jnp.int32)

def moe_segment(moe_input, norm_gain, routes, route_scores, w_up, w_down):
    input_wide = moe_input.astype(jnp.float32)
    inv_rms = 1.0 / jnp.sqrt(lax.optimization_barrier(jnp.mean(input_wide * input_wide, axis=1)) + NORM_EPSILON)
    scaled = (input_wide * norm_gain[None, :]).astype(jnp.bfloat16)
    signal = jax.nn.sigmoid(route_scores)
    gate_values = settle(signal / lax.optimization_barrier(jnp.sum(signal, axis=1, keepdims=True)))
    blocks = routes.reshape(N_EXPERT, TOK_DEV, TOPK).astype(jnp.int32)
    places = jax.vmap(slot_places)(blocks)
    column = jnp.arange(N_EXPERT, dtype=jnp.int32)[:, None, None]
    token_index = column * TOK_DEV + jnp.arange(TOK_DEV, dtype=jnp.int32)[None, :, None]
    token_index = jnp.broadcast_to(token_index, blocks.shape).astype(jnp.int32)
    slot_index = (column * CAP + places).astype(jnp.int32)
    row_table = jnp.zeros((EXPERTS, N_EXPERT * CAP), jnp.int32).at[blocks, slot_index].set(token_index)
    weight = jnp.zeros((EXPERTS, N_EXPERT * CAP), jnp.float32).at[blocks, slot_index].set(gate_values.reshape(blocks.shape))
    feature_block = D // N_DP

    def per_expert(combined, inputs):
        rows_index, gate_column, up_matrix, down_matrix = inputs
        gathered = scaled[rows_index].astype(jnp.float32)
        pieces = jnp.einsum('rbw,bwh->rbh', gathered.reshape(-1, N_DP, feature_block), up_matrix.reshape(N_DP, feature_block, HID).astype(jnp.float32))
        projected = lax.optimization_barrier(jnp.sum(settle(pieces), axis=1)) * inv_rms[rows_index][:, None]
        hidden = jnp.square(jnp.maximum(projected, 0.0)).astype(jnp.bfloat16)
        expert_out = settle(jnp.dot(hidden, down_matrix, preferred_element_type=jnp.float32))
        return (combined.at[rows_index].add(gate_column[:, None] * expert_out), None)
    combined, _ = lax.scan(per_expert, jnp.zeros((TOKENS, D), jnp.float32), (row_table, weight, w_up, w_down))
    return combined.astype(jnp.bfloat16)

def attention_segment(queries, keys, values, out_grad, w_query, w_key, w_value, w_out):
    sequences = TOKENS // TOK_DEV
    group_size = HEADS // KV_HEADS
    score_scale = HEAD_DIM ** (-0.5)
    d_attn = jnp.dot(out_grad, w_out.T, preferred_element_type=jnp.float32).astype(jnp.bfloat16)
    query_heads = queries.reshape(sequences, TOK_DEV, HEADS, HEAD_DIM).astype(jnp.float32)
    key_heads = jnp.repeat(keys.reshape(sequences, TOK_DEV, KV_HEADS, HEAD_DIM), group_size, axis=2).astype(jnp.float32)
    value_heads = jnp.repeat(values.reshape(sequences, TOK_DEV, KV_HEADS, HEAD_DIM), group_size, axis=2).astype(jnp.float32)
    grad_heads = d_attn.reshape(sequences, TOK_DEV, HEADS, HEAD_DIM).astype(jnp.float32)
    scores = jnp.einsum('sihd,sjhd->shij', query_heads, key_heads) * score_scale
    positions = jnp.arange(TOK_DEV, dtype=jnp.int32)
    causal = positions[None, :] <= positions[:, None]
    scores = jnp.where(causal[None, None], scores, -jnp.inf)
    peak = lax.optimization_barrier(jnp.max(scores, axis=-1, keepdims=True))
    raised = jnp.exp(scores - peak)
    attn_weights = raised / lax.optimization_barrier(jnp.sum(raised, axis=-1, keepdims=True))
    d_weights = jnp.einsum('sihd,sjhd->shij', grad_heads, value_heads)
    row_delta = lax.optimization_barrier(jnp.sum(attn_weights * d_weights, axis=-1, keepdims=True))
    d_scores = settle(attn_weights * (d_weights - row_delta))
    d_query = settle(jnp.einsum('shij,sjhd->sihd', d_scores, key_heads) * score_scale)
    d_key = jnp.einsum('shij,sihd->sjhd', d_scores, query_heads) * score_scale
    d_value = jnp.einsum('shij,sihd->sjhd', settle(attn_weights), grad_heads)
    combined = jnp.zeros((TOKENS, D), jnp.float32)
    for block_index in range(HEADS // HEAD_BLOCK):
        first_head = block_index * HEAD_BLOCK
        head_group = first_head // group_size
        block_query = d_query[:, :, first_head:first_head + HEAD_BLOCK].reshape(TOKENS, HEAD_BLOCK * HEAD_DIM)
        block_key = settle(lax.optimization_barrier(jnp.sum(d_key[:, :, first_head:first_head + HEAD_BLOCK], axis=2))).reshape(TOKENS, HEAD_DIM)
        block_value = settle(lax.optimization_barrier(jnp.sum(d_value[:, :, first_head:first_head + HEAD_BLOCK], axis=2))).reshape(TOKENS, HEAD_DIM)
        query_cols = w_query[:, first_head * HEAD_DIM:(first_head + HEAD_BLOCK) * HEAD_DIM]
        key_cols = w_key[:, head_group * HEAD_DIM:(head_group + 1) * HEAD_DIM]
        value_cols = w_value[:, head_group * HEAD_DIM:(head_group + 1) * HEAD_DIM]
        grad_term = jnp.dot(block_query.astype(jnp.bfloat16), query_cols.T, preferred_element_type=jnp.float32)
        grad_term = grad_term + jnp.dot(block_key.astype(jnp.bfloat16), key_cols.T, preferred_element_type=jnp.float32)
        grad_term = grad_term + jnp.dot(block_value.astype(jnp.bfloat16), value_cols.T, preferred_element_type=jnp.float32)
        combined = combined + settle(grad_term)
    return combined.astype(jnp.bfloat16)

def reference(moe_input, norm_gain, routes, route_scores, w_up, w_down, queries, keys, values, out_grad, w_query, w_key, w_value, w_out):
    moe_parts = [moe_segment(moe_input[segment_index], norm_gain, routes[segment_index], route_scores[segment_index], w_up, w_down) for segment_index in range(SEGMENTS)]
    grad_parts = [attention_segment(queries[segment_index], keys[segment_index], values[segment_index], out_grad[segment_index], w_query, w_key, w_value, w_out) for segment_index in range(SEGMENTS)]
    return (jnp.stack(moe_parts[::-1]), jnp.stack(grad_parts[::-1]))
```

```python
import jax
import jax.numpy as jnp
from jax import lax
from jax.sharding import PartitionSpec as P

D = 2688
HEADS = 16
KV_HEADS = 2
HEAD_DIM = 128
TOPK = 6
NORM_EPSILON = 1e-05


def relative(index, step, count):
    return index ^ step if count & (count - 1) == 0 else (index + step) % count


def fetch(block, axis, pairs):
    return lax.ppermute(block, axis, pairs)


def dp_pairs(step):
    count = lax.axis_size("dp")
    return [(relative(i, step, count), i) for i in range(count)]


def expert_pairs(rows_step, fast_step, back=False):
    columns = lax.axis_size("expert")
    fast_count = 2 if columns % 2 == 0 else 1
    slow_count = columns // fast_count
    pairs = []
    for slow in range(slow_count):
        for fast in range(fast_count):
            source = relative(slow, rows_step, slow_count) * fast_count + relative(
                fast, fast_step, fast_count
            )
            here = slow * fast_count + fast
            pairs.append((here, source) if back else (source, here))
    return pairs


def crossed(pairs, other_axis_count):
    return [
        (segment * other_axis_count + a, (1 - segment) * other_axis_count + b)
        for segment in range(2)
        for a, b in pairs
    ]


def attention_grad(queries, keys, values, out_grad, w_query, w_key, w_value, w_out, block_index):
    token_count = queries.shape[0]
    query_width = queries.shape[1]
    heads_here = query_width // HEAD_DIM
    group_size = HEADS // KV_HEADS
    score_scale = HEAD_DIM ** (-0.5)
    head_group = block_index * heads_here // group_size
    kv_start = head_group * HEAD_DIM
    key_head = lax.dynamic_slice_in_dim(keys, kv_start, HEAD_DIM, 1)
    value_head = lax.dynamic_slice_in_dim(values, kv_start, HEAD_DIM, 1)
    key_weight = lax.dynamic_slice_in_dim(w_key, kv_start, HEAD_DIM, 1)
    value_weight = lax.dynamic_slice_in_dim(w_value, kv_start, HEAD_DIM, 1)
    d_attn = jnp.einsum("td,qd->tq", out_grad, w_out, preferred_element_type=jnp.float32).astype(
        jnp.bfloat16
    )
    grad_heads = d_attn.reshape(token_count, heads_here, HEAD_DIM)
    query_heads = queries.reshape(token_count, heads_here, HEAD_DIM)
    scores = (
        jnp.einsum("ihd,jd->hij", query_heads, key_head, preferred_element_type=jnp.float32)
        * score_scale
    )
    positions = jnp.arange(token_count, dtype=jnp.int32)
    causal = positions[None, :] <= positions[:, None]
    scores = jnp.where(causal[None], scores, -jnp.inf)
    peak = jnp.max(scores, axis=2, keepdims=True)
    raised = jnp.exp(scores - peak)
    attn_weights = raised / jnp.sum(raised, axis=2, keepdims=True)
    d_weights = jnp.einsum(
        "ihd,jd->hij", grad_heads, value_head, preferred_element_type=jnp.float32
    )
    row_delta = jnp.sum(attn_weights * d_weights, axis=2, keepdims=True)
    d_scores = (attn_weights * (d_weights - row_delta)).astype(jnp.bfloat16)
    d_query = (
        jnp.einsum("hij,jd->ihd", d_scores, key_head, preferred_element_type=jnp.float32)
        * score_scale
    )
    d_query = d_query.astype(jnp.bfloat16).reshape(token_count, query_width)
    d_key = (
        jnp.einsum("hij,ihd->jd", d_scores, query_heads, preferred_element_type=jnp.float32)
        * score_scale
    ).astype(jnp.bfloat16)
    d_value = jnp.einsum(
        "hij,ihd->jd",
        attn_weights.astype(jnp.bfloat16),
        grad_heads,
        preferred_element_type=jnp.float32,
    ).astype(jnp.bfloat16)
    grad_term = jnp.einsum("tq,dq->td", d_query, w_query, preferred_element_type=jnp.float32)
    grad_term = grad_term + jnp.einsum(
        "tk,dk->td", d_key, key_weight, preferred_element_type=jnp.float32
    )
    grad_term = grad_term + jnp.einsum(
        "tk,dk->td", d_value, value_weight, preferred_element_type=jnp.float32
    )
    return grad_term.astype(jnp.bfloat16)


def gather_tokens(own):
    columns = lax.axis_size("expert")
    dp_count = lax.axis_size("dp")
    fast_count = 2 if columns % 2 == 0 else 1
    slow_count = columns // fast_count
    parts = [dict() for _ in range(dp_count)]
    for slow in range(slow_count):
        parts[0][0, slow] = own if slow == 0 else fetch(own, "expert", expert_pairs(slow, 0))

    def over_dp(block, step):
        return fetch(block, "dp", dp_pairs(step))

    def over_fast(block):
        return fetch(block, "expert", expert_pairs(0, 1))

    groups = [[0], [1], list(range(2, slow_count))]
    pending = []
    for group in groups:
        group = [slow for slow in group if slow < slow_count]
        if not group:
            continue
        block = jnp.concatenate([parts[0][0, slow] for slow in group], axis=0)
        rows = own.shape[0]
        cut = lambda whole, i: whole[i * rows : (i + 1) * rows]
        for step in range(1, dp_count):
            moved = over_dp(block, step)
            for i, slow in enumerate(group):
                parts[step][0, slow] = cut(moved, i)
        if fast_count == 2:
            moved = over_fast(block)
            for i, slow in enumerate(group):
                parts[0][1, slow] = cut(moved, i)
    if fast_count == 2:
        for first in range(0, slow_count, 2):
            for slow in range(first, min(first + 2, slow_count)):
                for step in range(1, dp_count):
                    if dp_count == 2 and slow % 2 == 1:
                        parts[step][1, slow] = over_fast(parts[step][0, slow])
                    else:
                        parts[step][1, slow] = over_dp(parts[0][1, slow], step)
    return parts


def on_device(
    moe_input,
    norm_gain,
    routes,
    route_scores,
    w_up,
    w_down,
    queries,
    keys,
    values,
    out_grad,
    w_query,
    w_key,
    w_value,
    w_out,
):
    columns = lax.axis_size("expert")
    dp_count = lax.axis_size("dp")
    fast_count = 2 if columns % 2 == 0 else 1
    slow_count = columns // fast_count
    token_count = moe_input.shape[1]
    feature_share = moe_input.shape[2]
    local_experts = w_up.shape[0]
    hidden_share = w_up.shape[2]
    expert_count = local_experts * columns
    capacity = (9 * token_count * TOPK + 8 * expert_count - 1) // (8 * expert_count)
    slot_count = columns * capacity
    feature_index = lax.axis_index("dp")
    place = lax.axis_index("expert")

    signal = jax.nn.sigmoid(route_scores[0])
    gate_values = (
        (signal / jnp.sum(signal, axis=1, keepdims=True)).astype(jnp.bfloat16).astype(jnp.float32)
    )
    expert_ids = jnp.arange(expert_count, dtype=jnp.int32)
    gate_table = jnp.full((expert_count, token_count), -1.0, jnp.float32)
    for choice in range(TOPK):
        gate_table = jnp.where(
            expert_ids[:, None] == routes[0][None, :, choice],
            gate_values[None, :, choice],
            gate_table,
        )
    arrived = lax.all_to_all(
        gate_table.reshape(columns, local_experts, token_count),
        "expert",
        split_axis=0,
        concat_axis=0,
        tiled=True,
    )

    parts = gather_tokens(moe_input[0])
    order = [(fast, slow) for fast in range(fast_count) for slow in range(slow_count)]

    grad_term = attention_grad(
        queries[0], keys[0], values[0], out_grad[0], w_query, w_key, w_value, w_out, feature_index
    )

    sources = []
    for fast, slow in order:
        slow_here, fast_here = place // fast_count, place % fast_count
        if slow_count & (slow_count - 1) == 0:
            slow_there = slow_here ^ slow
        else:
            slow_there = (slow_here + slow) % slow_count
        fast_there = fast_here ^ fast
        sources.append(slow_there * fast_count + fast_there)
    gates = jnp.concatenate(
        [lax.dynamic_slice_in_dim(arrived, source, 1, 0)[0] for source in sources], axis=1
    )
    member = gates >= 0
    positions = jnp.cumsum(member.astype(jnp.int32), axis=1) - 1
    positions = jnp.where(member, positions, -1)
    slot_ids = jnp.arange(slot_count, dtype=jnp.int32)

    tokens = [
        jnp.concatenate([parts[step][key] for key in order], axis=0) for step in range(dp_count)
    ]
    hidden_parts = []
    for expert in range(local_experts):
        pick = (slot_ids[:, None] == positions[expert][None, :]).astype(jnp.bfloat16)
        running = jnp.zeros((slot_count, hidden_share), jnp.float32)
        squares = jnp.zeros((slot_count,), jnp.float32)
        for step in range(dp_count):
            if dp_count & (dp_count - 1) == 0:
                share = feature_index ^ step
            else:
                share = (feature_index + step) % dp_count
            start = share * feature_share
            rows = jnp.dot(pick, tokens[step], preferred_element_type=jnp.float32)
            squares = squares + jnp.sum(jnp.square(rows), axis=1)
            gain = lax.dynamic_slice_in_dim(norm_gain, start, feature_share, 0)
            scaled = (rows * gain[None, :]).astype(jnp.bfloat16)
            weight = lax.dynamic_slice_in_dim(w_up[expert], start, feature_share, 0)
            running = running + jnp.dot(scaled, weight, preferred_element_type=jnp.float32).astype(
                jnp.bfloat16
            ).astype(jnp.float32)
        inverse = 1.0 / jnp.sqrt(squares / D + NORM_EPSILON)
        projected = running * inverse[:, None]
        hidden = jnp.square(jnp.maximum(projected, 0.0)).astype(jnp.bfloat16)
        pieces = [hidden] + [
            fetch(hidden, "dp", dp_pairs(step)) for step in range(1, dp_count)
        ]
        hidden_parts.append(pieces)

    partial = None
    for expert in range(local_experts):
        total = None
        for step in range(dp_count):
            if dp_count & (dp_count - 1) == 0:
                share = feature_index ^ step
            else:
                share = (feature_index + step) % dp_count
            weight = lax.dynamic_slice_in_dim(
                w_down[expert], share * hidden_share, hidden_share, 0
            )
            term = jnp.dot(hidden_parts[expert][step], weight, preferred_element_type=jnp.float32)
            total = term if total is None else total + term
        expert_rows = total.astype(jnp.bfloat16)
        mixing = jnp.where(
            slot_ids[None, :] == positions[expert][:, None], gates[expert][:, None], 0.0
        ).astype(jnp.bfloat16)
        term = jnp.dot(mixing, expert_rows, preferred_element_type=jnp.float32)
        partial = term if partial is None else partial + term
    partial = partial.reshape(fast_count, slow_count, token_count, feature_share)

    def swap(block):
        return lax.ppermute(block, "segment", [(0, 1), (1, 0)])

    def cross_expert(block, rows_step, fast_step):
        return lax.ppermute(
            block,
            ("segment", "expert"),
            crossed(expert_pairs(rows_step, fast_step, back=True), columns),
        )

    cut = token_count * 5 // 8 if fast_count == 2 else token_count
    head = partial[:, :, :cut].astype(jnp.bfloat16)
    near = partial[0, :, :cut]
    if fast_count == 2:
        near = near + fetch(head[1], "expert", expert_pairs(0, 1)).astype(jnp.float32)
    near = near.astype(jnp.bfloat16)
    head_sum = swap(near[0]).astype(jnp.float32)
    tail_sum = partial[:, 0, cut:]
    tail = partial[:, :, cut:].astype(jnp.bfloat16)
    if fast_count == 2:
        for slow in range(1, slow_count):
            moved = fetch(tail[:, slow], "expert", expert_pairs(slow, 0, back=True))
            tail_sum = tail_sum + moved.astype(jnp.float32)
    for slow in range(1, slow_count):
        head_sum = head_sum + cross_expert(near[slow], slow, 0).astype(jnp.float32)
    moe_next = head_sum.astype(jnp.bfloat16)
    if fast_count == 2:
        tail_sum = tail_sum.astype(jnp.bfloat16)
        last = swap(tail_sum[0]).astype(jnp.float32) + cross_expert(tail_sum[1], 0, 1).astype(
            jnp.float32
        )
        moe_next = jnp.concatenate([moe_next, last.astype(jnp.bfloat16)], axis=0)

    grad_sum = None
    for step in range(dp_count):
        if dp_count & (dp_count - 1) == 0:
            share = feature_index ^ step
            pairs = [(i, i ^ step) for i in range(dp_count)]
        else:
            share = (feature_index + step) % dp_count
            pairs = [(i, (i + step) % dp_count) for i in range(dp_count)]
        piece = lax.dynamic_slice_in_dim(grad_term, share * feature_share, feature_share, 1)
        moved = lax.ppermute(piece, ("segment", "dp"), crossed(pairs, dp_count)).astype(
            jnp.float32
        )
        grad_sum = moved if grad_sum is None else grad_sum + moved
    grad_prev = grad_sum.astype(jnp.bfloat16)
    return (moe_next[None], grad_prev[None])


def solution(mesh):
    return jax.shard_map(
        on_device,
        mesh=mesh,
        in_specs=(
            P("segment", "expert", "dp"),
            P(),
            P("segment", "expert", None),
            P("segment", "expert", None),
            P("expert", None, "dp"),
            P("expert", None, "dp"),
            P("segment", "expert", "dp"),
            P("segment", "expert", None),
            P("segment", "expert", None),
            P("segment", "expert", None),
            P(None, "dp"),
            P(),
            P(),
            P("dp", None),
        ),
        out_specs=(P("segment", "expert", "dp"), P("segment", "expert", "dp")),
        check_vma=False,
    )
```

```python
import functools

import jax
import jax.numpy as jnp
from jax import lax
from jax.experimental import pallas as pl
from jax.experimental.pallas import tpu as pltpu
from jax.sharding import PartitionSpec as P

D = 2688
HEADS = 16
KV_HEADS = 2
HEAD_DIM = 128
TOPK = 6
NORM_EPSILON = 1e-05


def relative(index, step, count):
    return index ^ step if count & (count - 1) == 0 else (index + step) % count


def relative_traced(index, step, count):
    return index ^ step if count & (count - 1) == 0 else (index + step) % count


def dp_pairs(step):
    count = lax.axis_size("dp")
    return [(relative(i, step, count), i) for i in range(count)]


def expert_pairs(rows_step, fast_step, back=False):
    columns = lax.axis_size("expert")
    fast_count = 2 if columns % 2 == 0 else 1
    slow_count = columns // fast_count
    pairs = []
    for slow in range(slow_count):
        for fast in range(fast_count):
            source = relative(slow, rows_step, slow_count) * fast_count + relative(
                fast, fast_step, fast_count
            )
            here = slow * fast_count + fast
            pairs.append((here, source) if back else (source, here))
    return pairs


def crossed(pairs, other_axis_count):
    return [
        (segment * other_axis_count + a, (1 - segment) * other_axis_count + b)
        for segment in range(2)
        for a, b in pairs
    ]


def attention_grad(queries, keys, values, out_grad, w_query, w_key, w_value, w_out, block_index):
    token_count = queries.shape[0]
    query_width = queries.shape[1]
    heads_here = query_width // HEAD_DIM
    group_size = HEADS // KV_HEADS
    score_scale = HEAD_DIM ** (-0.5)
    head_group = block_index * heads_here // group_size
    kv_start = head_group * HEAD_DIM
    key_head = lax.dynamic_slice_in_dim(keys, kv_start, HEAD_DIM, 1)
    value_head = lax.dynamic_slice_in_dim(values, kv_start, HEAD_DIM, 1)
    key_weight = lax.dynamic_slice_in_dim(w_key, kv_start, HEAD_DIM, 1)
    value_weight = lax.dynamic_slice_in_dim(w_value, kv_start, HEAD_DIM, 1)
    d_attn = jnp.einsum("td,qd->tq", out_grad, w_out, preferred_element_type=jnp.float32).astype(
        jnp.bfloat16
    )
    grad_heads = d_attn.reshape(token_count, heads_here, HEAD_DIM)
    query_heads = queries.reshape(token_count, heads_here, HEAD_DIM)
    scores = (
        jnp.einsum("ihd,jd->hij", query_heads, key_head, preferred_element_type=jnp.float32)
        * score_scale
    )
    positions = jnp.arange(token_count, dtype=jnp.int32)
    causal = positions[None, :] <= positions[:, None]
    scores = jnp.where(causal[None], scores, -jnp.inf)
    peak = jnp.max(scores, axis=2, keepdims=True)
    raised = jnp.exp(scores - peak)
    attn_weights = raised / jnp.sum(raised, axis=2, keepdims=True)
    d_weights = jnp.einsum(
        "ihd,jd->hij", grad_heads, value_head, preferred_element_type=jnp.float32
    )
    row_delta = jnp.sum(attn_weights * d_weights, axis=2, keepdims=True)
    d_scores = (attn_weights * (d_weights - row_delta)).astype(jnp.bfloat16)
    d_query = (
        jnp.einsum("hij,jd->ihd", d_scores, key_head, preferred_element_type=jnp.float32)
        * score_scale
    )
    d_query = d_query.astype(jnp.bfloat16).reshape(token_count, query_width)
    d_key = (
        jnp.einsum("hij,ihd->jd", d_scores, query_heads, preferred_element_type=jnp.float32)
        * score_scale
    ).astype(jnp.bfloat16)
    d_value = jnp.einsum(
        "hij,ihd->jd",
        attn_weights.astype(jnp.bfloat16),
        grad_heads,
        preferred_element_type=jnp.float32,
    ).astype(jnp.bfloat16)
    grad_term = jnp.einsum("tq,dq->td", d_query, w_query, preferred_element_type=jnp.float32)
    grad_term = grad_term + jnp.einsum(
        "tk,dk->td", d_key, key_weight, preferred_element_type=jnp.float32
    )
    grad_term = grad_term + jnp.einsum(
        "tk,dk->td", d_value, value_weight, preferred_element_type=jnp.float32
    )
    return grad_term.astype(jnp.bfloat16)


AHEAD = 2


def tile_starts(length):
    count = 2 if length % 16 == 0 and (length // 2) % 16 == 0 else 1
    units = length // 16
    return [units * i // count * 16 for i in range(count)] + [length]


def weight_copies(weight, held, sems):
    starts = tile_starts(held.shape[1])
    return [
        (
            expert,
            slice(first, last),
            pltpu.make_async_copy(
                weight.at[expert, pl.ds(first, last - first)],
                held.at[expert, pl.ds(first, last - first)],
                sems.at[expert * (len(starts) - 1) + i],
            ),
        )
        for expert in range(held.shape[0])
        for i, (first, last) in enumerate(zip(starts, starts[1:]))
    ]


def slot_tables(gates_ref, order, blocks, groups, group_width):
    experts, block = gates_ref.shape[1:]
    before = lax.broadcasted_iota(jnp.int32, (block, block), 0)
    here = lax.broadcasted_iota(jnp.int32, (block, block), 1)
    counted = jnp.where(before <= here, 1.0, 0.0).astype(jnp.bfloat16)
    expert = lax.broadcasted_iota(jnp.int32, (experts, block), 0)
    all_gates, all_places = [], []
    for i, index in enumerate(blocks):
        group, first = divmod(i, len(blocks) // groups)
        if first == 0:
            taken = expert * group_width * groups + group * group_width
        gates = gates_ref[order[index]]
        member = gates >= 0
        ones = jnp.where(member, 1.0, 0.0)
        count = jnp.dot(
            ones.astype(jnp.bfloat16), counted, preferred_element_type=jnp.float32
        ).astype(jnp.int32)
        all_gates.append(gates)
        all_places.append(jnp.where(member, taken + count - 1, -1))
        taken = taken + jnp.sum(ones, axis=1, keepdims=True).astype(jnp.int32)
    return jnp.concatenate(all_gates, axis=1), jnp.concatenate(all_places, axis=1)


def up_kernel(shares, order, gates_ref, gain_ref, weight, *rest, blocks, groups):
    (*pieces_and_outs, held, tokens, scaled, gains, squares, weight_sems, piece_sems) = rest
    pieces, outs = pieces_and_outs[:-groups], pieces_and_outs[-groups:]
    block_count = len(blocks)
    dp_count, share_rows, token_count = tokens.shape
    experts = held.shape[0]
    width = scaled.shape[1] // experts
    lanes_of = pieces[0].shape[1]
    loads = [
        pltpu.make_async_copy(
            piece,
            tokens.at[i // block_count, :, pl.ds(i % block_count * lanes_of, lanes_of)],
            piece_sems.at[i],
        )
        for i, piece in enumerate(pieces)
    ]
    weights = weight_copies(weight, held, weight_sems)
    for load in loads:
        load.start()

    for i in range(gain_ref.shape[0]):
        column = jnp.broadcast_to(gain_ref[i : i + 1, :], (128, 128)).T
        gains[i * 128 : (i + 1) * 128, :] = column
    _, places = slot_tables(gates_ref, order, blocks, groups, width // groups)
    slot = lax.broadcasted_iota(jnp.int32, (experts * width, token_count), 0)
    pick = slot == places[0:1, :]
    for other in range(1, experts):
        pick = pick | (slot == places[other : other + 1, :])
    pick = jnp.where(pick, 1.0, 0.0).astype(jnp.bfloat16)
    squares[...] = jnp.zeros_like(squares)
    chunk = share_rows
    for step in range(dp_count):
        for load in loads[step * block_count : (step + 1) * block_count]:
            load.wait()
        if step == 0:
            for _, _, load in weights[:AHEAD]:
                load.start()

        @pl.loop(0, share_rows // chunk)
        def _(i):
            rows = pl.ds(pl.multiple_of(i * chunk, 16), chunk)
            picked = lax.dot_general(
                tokens[step, rows, :],
                pick,
                (((1,), (1,)), ((), ())),
                preferred_element_type=jnp.float32,
            )
            squares[...] = squares[...] + jnp.sum(picked * picked, axis=0, keepdims=True)
            place = pl.ds(pl.multiple_of(shares[step] * share_rows + i * chunk, 16), chunk)
            gain = jnp.concatenate([gains[place, :]] * (experts * width // 128), axis=1)
            scaled[place, :] = (picked * gain).astype(jnp.bfloat16)

    group_width = width // groups
    for i, (expert, rows, load) in enumerate(weights):
        lanes = slice(expert * width, (expert + 1) * width)
        inverse = 1.0 / jnp.sqrt(squares[:, lanes] / D + NORM_EPSILON)
        load.wait()
        if i + AHEAD < len(weights):
            weights[i + AHEAD][2].start()
        product = jnp.dot(
            held[expert, rows, :], scaled[:, lanes], preferred_element_type=jnp.float32
        )
        value = jnp.square(jnp.maximum(product * inverse, 0.0)).astype(jnp.bfloat16)
        for group, out in enumerate(outs):
            out[rows, expert * group_width : (expert + 1) * group_width] = value[
                :, group * group_width : (group + 1) * group_width
            ]


def up_chunk(parts, groups, columns, order, gates, gain, weight, shares, group_width):
    experts, hidden_share, features = weight.shape
    keys = [key for group in groups for key in group]
    pieces = [part[key] for part in parts for key in keys]
    share_rows, block = pieces[0].shape
    tokens = len(keys) * block
    slots = experts * group_width * len(groups)
    vmem, anywhere = pl.BlockSpec(memory_space=pltpu.VMEM), pl.BlockSpec(memory_space=pl.ANY)
    smem = pl.BlockSpec(memory_space=pltpu.SMEM)
    blocks = tuple(columns[key] for key in keys)
    return pl.pallas_call(
        functools.partial(up_kernel, blocks=blocks, groups=len(groups)),
        out_shape=[
            jax.ShapeDtypeStruct((hidden_share, experts * group_width), jnp.bfloat16)
            for _ in groups
        ],
        in_specs=[smem, smem, vmem, vmem, anywhere] + [anywhere] * len(pieces),
        out_specs=[vmem] * len(groups),
        scratch_shapes=[
            pltpu.VMEM(weight.shape, jnp.bfloat16),
            pltpu.VMEM((len(parts), share_rows, tokens), jnp.bfloat16),
            pltpu.VMEM((features, slots), jnp.bfloat16),
            pltpu.VMEM((features, 128), jnp.float32),
            pltpu.VMEM((1, slots), jnp.float32),
            pltpu.SemaphoreType.DMA((experts * (len(tile_starts(hidden_share)) - 1),)),
            pltpu.SemaphoreType.DMA((len(pieces),)),
        ],
        cost_estimate=pl.CostEstimate(
            flops=2 * slots * features * (tokens + hidden_share),
            bytes_accessed=2 * (weight.size + tokens * features + slots * hidden_share),
            transcendentals=0,
        ),
    )(shares, order, gates, gain, weight, *pieces)


def down_kernel(shares, order, gates_ref, weight, *rest, dp_count, blocks, heads):
    pieces, outs = rest[:dp_count], rest[dp_count:-5]
    held, hidden, collected, weight_sems, piece_sems = rest[-5:]
    experts = held.shape[0]
    width = hidden.shape[1] // experts
    piece_rows = pieces[0].shape[0]
    loads = []
    for step, piece in enumerate(pieces):
        start = 0 if dp_count == 1 else pl.multiple_of(shares[step] * piece_rows, 16)
        loads.append(
            pltpu.make_async_copy(
                piece, hidden.at[pl.ds(start, piece_rows), :], piece_sems.at[step]
            )
        )
    weights = weight_copies(weight, held, weight_sems)
    for load in loads:
        load.start()
    for _, _, load in weights[:AHEAD]:
        load.start()

    gates, places = slot_tables(gates_ref, order, blocks, 1, width)
    token_count = gates.shape[1]
    slot = lax.broadcasted_iota(jnp.int32, (experts * width, token_count), 0)
    mixing = jnp.zeros((experts * width, token_count), jnp.float32)
    for expert in range(experts):
        row = slice(expert, expert + 1)
        mixing = jnp.where(slot == places[row, :], gates[row, :], mixing)
    mixing = mixing.astype(jnp.bfloat16)
    for load in loads:
        load.wait()
    half = collected.shape[0] // 2
    block = token_count // len(blocks)
    for i, (expert, rows, load) in enumerate(weights):
        lanes = slice(expert * width, (expert + 1) * width)
        load.wait()
        if i + AHEAD < len(weights):
            weights[i + AHEAD][2].start()
        collected[rows, lanes] = jnp.dot(
            held[expert, rows, :], hidden[:, lanes], preferred_element_type=jnp.float32
        ).astype(jnp.bfloat16)
        if expert < experts - 1:
            continue
        partial = jnp.dot(collected[rows, :], mixing, preferred_element_type=jnp.float32)
        first, middle, last = rows.start, min(max(half, rows.start), rows.stop), rows.stop
        if first < middle:
            share = token_count // heads
            for j, out in enumerate(outs[:heads]):
                out[first:middle] = partial[: middle - first, j * share : (j + 1) * share].astype(
                    out.dtype
                )
        if middle < last:
            for j, out in enumerate(outs[heads:]):
                out[middle - half : last - half] = partial[
                    middle - first :, j * block : (j + 1) * block
                ].astype(out.dtype)


def down_chunk(pieces, keys, columns, order, gates, weight, shares, heads):
    experts, feature_share, hidden_units = weight.shape
    if len(pieces) > 1 and pieces[0].shape[0] % 16:
        joined = jnp.zeros((hidden_units, pieces[0].shape[1]), jnp.bfloat16)
        for step, piece in enumerate(pieces):
            joined = lax.dynamic_update_slice_in_dim(
                joined, piece, shares[step] * piece.shape[0], 0
            )
        pieces = [joined]
    slots = pieces[0].shape[1]
    block = gates.shape[2]
    tokens = len(keys) * block
    half = feature_share // 2
    outs = [((half, tokens // heads), jnp.float32 if keys[0][0] == 0 else jnp.bfloat16)] * heads
    outs += [
        ((half, block), jnp.float32 if slow == 0 else jnp.bfloat16) for _, slow in keys
    ]
    vmem, anywhere = pl.BlockSpec(memory_space=pltpu.VMEM), pl.BlockSpec(memory_space=pl.ANY)
    smem = pl.BlockSpec(memory_space=pltpu.SMEM)
    blocks = tuple(columns[key] for key in keys)
    results = pl.pallas_call(
        functools.partial(down_kernel, dp_count=len(pieces), blocks=blocks, heads=heads),
        out_shape=[jax.ShapeDtypeStruct(shape, dtype) for shape, dtype in outs],
        in_specs=[smem, smem, vmem, anywhere] + [anywhere] * len(pieces),
        out_specs=[vmem] * len(outs),
        scratch_shapes=[
            pltpu.VMEM(weight.shape, jnp.bfloat16),
            pltpu.VMEM((hidden_units, slots), jnp.bfloat16),
            pltpu.VMEM((feature_share, slots), jnp.bfloat16),
            pltpu.SemaphoreType.DMA((experts * (len(tile_starts(feature_share)) - 1),)),
            pltpu.SemaphoreType.DMA((len(pieces),)),
        ],
        cost_estimate=pl.CostEstimate(
            flops=2 * slots * feature_share * (tokens + hidden_units),
            bytes_accessed=2 * (weight.size + slots * hidden_units + 2 * tokens * feature_share),
            transcendentals=0,
        ),
    )(shares, order, gates, weight, *pieces)
    return results[:heads], dict(zip(keys, results[heads:]))


def gather_tokens(own):
    dp_count = lax.axis_size("dp")
    slow_count = lax.axis_size("expert") // 2
    parts = [dict() for _ in range(dp_count)]
    parts[0][0, 0] = own
    if slow_count == 4:
        def hop(block, moves):
            pairs = [(a * 2 + fast, b * 2 + fast) for a, b in moves for fast in range(2)]
            return lax.ppermute(block, "expert", pairs)

        inward, outward = [(1, 2), (2, 1)], [(1, 0), (2, 3)]
        parts[0][0, 1] = lax.ppermute(own, "expert", expert_pairs(1, 0))
        middle = hop(own, inward)
        beyond = hop(parts[0][0, 1], inward)
        parts[0][0, 2] = hop(middle, outward) + beyond
        parts[0][0, 3] = hop(beyond, outward) + middle
    else:
        for slow in range(1, slow_count):
            parts[0][0, slow] = lax.ppermute(own, "expert", expert_pairs(slow, 0))
    for slow in range(slow_count):
        block = parts[0][0, slow]
        for step in range(1, dp_count):
            parts[step][0, slow] = lax.ppermute(block, "dp", dp_pairs(step))
        parts[0][1, slow] = lax.ppermute(block, "expert", expert_pairs(0, 1))
    for slow in range(slow_count):
        for step in range(1, dp_count):
            if slow % 2 == 0:
                parts[step][1, slow] = lax.ppermute(parts[0][1, slow], "dp", dp_pairs(step))
            else:
                parts[step][1, slow] = lax.ppermute(
                    parts[step][0, slow], "expert", expert_pairs(0, 1)
                )
    return parts


def on_device(
    moe_input,
    norm_gain,
    routes,
    route_scores,
    w_up,
    w_down,
    queries,
    keys,
    values,
    out_grad,
    w_query,
    w_key,
    w_value,
    w_out,
):
    columns = lax.axis_size("expert")
    dp_count = lax.axis_size("dp")
    fast_count = 2
    slow_count = columns // fast_count
    token_count = moe_input.shape[1]
    feature_share = moe_input.shape[2]
    local_experts = w_up.shape[0]
    expert_count = local_experts * columns
    capacity = (9 * token_count * TOPK + 8 * expert_count - 1) // (8 * expert_count)
    feature_index = lax.axis_index("dp")
    place = lax.axis_index("expert")
    shares = jnp.stack([relative_traced(feature_index, d, dp_count) for d in range(dp_count)])

    parts = gather_tokens(moe_input[0].T)

    signal = jax.nn.sigmoid(route_scores[0])
    gate_values = (
        (signal / jnp.sum(signal, axis=1, keepdims=True)).astype(jnp.bfloat16).astype(jnp.float32)
    )
    expert_ids = jnp.arange(expert_count, dtype=jnp.int32)
    gate_table = jnp.full((expert_count, token_count), -1.0, jnp.float32)
    for choice in range(TOPK):
        gate_table = jnp.where(
            expert_ids[:, None] == routes[0][None, :, choice],
            gate_values[None, :, choice],
            gate_table,
        )
    arrived = lax.all_to_all(
        gate_table.reshape(columns, local_experts, token_count),
        "expert",
        split_axis=0,
        concat_axis=0,
        tiled=True,
    )

    grad_term = attention_grad(
        queries[0], keys[0], values[0], out_grad[0], w_query, w_key, w_value, w_out, feature_index
    )
    grad_sum = None
    for step in range(dp_count):
        pairs = [(i, relative(i, step, dp_count)) for i in range(dp_count)]
        piece = lax.dynamic_slice_in_dim(
            grad_term, shares[step] * feature_share, feature_share, 1
        ).T
        moved = lax.ppermute(piece, ("segment", "dp"), crossed(pairs, dp_count)).astype(jnp.float32)
        grad_sum = moved if grad_sum is None else grad_sum + moved
    grad_prev = grad_sum.astype(jnp.bfloat16).T[None]

    gain = norm_gain.reshape(-1, 128)
    up_weight, down_weight = jnp.swapaxes(w_up, 1, 2), jnp.swapaxes(w_down, 1, 2)
    near_keys = [(0, slow) for slow in range(slow_count)]
    far_keys = [(1, slow) for slow in range(slow_count)]
    middle = slow_count // 2
    chunks = {"near": near_keys, "deep": far_keys[middle:], "last": far_keys[:middle]}
    columns_of = {key: i for i, key in enumerate(near_keys + far_keys)}
    order = jnp.stack(
        [
            relative_traced(place // fast_count, slow, slow_count) * fast_count
            + relative_traced(place % fast_count, fast, fast_count)
            for fast, slow in near_keys + far_keys
        ]
    )
    hidden = {}
    for name, names in (("near", ["near"]), ("far", ["far"])):
        groups = [near_keys if name == "near" else far_keys]
        width = -(-max(len(group) for group in groups) * capacity // 128) * 128
        outs = up_chunk(parts, groups, columns_of, order, arrived, gain, up_weight, shares, width)
        for group, here in zip(names, outs):
            hidden[group] = [here] + [
                lax.ppermute(here, "dp", dp_pairs(step)) for step in range(1, dp_count)
            ]
    heads, tails = {}, {}
    for name, keys in (("near", near_keys), ("far", far_keys)):
        heads[name], tail = down_chunk(
            hidden[name], keys, columns_of, order, arrived, down_weight, shares, 2
        )
        tails.update(tail)

    def cross_expert(block, rows_step, fast_step):
        pairs = crossed(expert_pairs(rows_step, fast_step, back=True), columns)
        return lax.ppermute(block, ("segment", "expert"), pairs).astype(jnp.float32)

    moved_heads = {
        name: lax.ppermute(head, "expert", expert_pairs(0, 1))
        for name, head in zip(("deep", "last"), heads["far"][::-1])
    }
    head_sum, near_sum, far_sum = None, tails[0, 0], tails[1, 0]
    for name, near_head in zip(("deep", "last"), heads["near"][::-1]):
        for i, (_, slow) in enumerate(chunks[name]):
            lanes = slice(i * token_count, (i + 1) * token_count)
            block = near_head[:, lanes] + moved_heads[name][:, lanes].astype(jnp.float32)
            moved = cross_expert(block.astype(jnp.bfloat16), slow, 0)
            head_sum = moved if head_sum is None else head_sum + moved
    for slow in reversed(range(1, slow_count)):
        pairs = expert_pairs(slow, 0, back=True)
        near_moved = lax.ppermute(tails[0, slow], "expert", pairs)
        far_moved = lax.ppermute(tails[1, slow], "expert", pairs)
        near_sum = near_sum + near_moved.astype(jnp.float32)
        far_sum = far_sum + far_moved.astype(jnp.float32)
    near_sum, far_sum = near_sum.astype(jnp.bfloat16), far_sum.astype(jnp.bfloat16)
    tail_sum = cross_expert(near_sum, 0, 0) + cross_expert(far_sum, 0, 1)
    moe_next = jnp.concatenate(
        [head_sum.astype(jnp.bfloat16), tail_sum.astype(jnp.bfloat16)], axis=0
    )
    return (moe_next.T[None], grad_prev)


def solution(mesh):
    return jax.shard_map(
        on_device,
        mesh=mesh,
        in_specs=(
            P("segment", "expert", "dp"),
            P(),
            P("segment", "expert", None),
            P("segment", "expert", None),
            P("expert", None, "dp"),
            P("expert", None, "dp"),
            P("segment", "expert", "dp"),
            P("segment", "expert", None),
            P("segment", "expert", None),
            P("segment", "expert", None),
            P(None, "dp"),
            P(),
            P(),
            P("dp", None),
        ),
        out_specs=(P("segment", "expert", "dp"), P("segment", "expert", "dp")),
        check_vma=False,
    )
```
